512 devices in a mesh: seq: 32 (over y, x, core), head: 16 (over z).
Axes of the slice: x: 4, y: 4, z: 16, core: 2. Of those that a mesh axis runs over, the one named last changes fastest.
Arguments:
- values: bfloat16 [16384, 8192], P('seq', 'head'), may hold values from -6 to 6
- group_keys: bfloat16 [16384, 8, 128], P(('seq', 'head')), may hold values from -0.5 to 0.5
- group_queries: bfloat16 [16384, 8, 128], P(('seq', 'head')), may hold values from -0.16992188 to 0.16992188
- level_table: int32 [128, 20], P('head'), may hold values from 1 to 4
- window_index: int32 [1], replicated, may hold values from 0 to 15
- prior_states: bfloat16 [4, 128, 64, 128], P(None, 'head'), may hold values from -100 to 100
- cotangent: bfloat16 [16384, 8192], P('seq', 'head'), may hold values from -6 to 6
Outputs:
- mixer_out: bfloat16 [16384, 8192], P('seq', 'head')
- grad_values: bfloat16 [16384, 8192], P('seq', 'head')
- grad_keys: float32 [16384, 8, 128], P(('seq', 'head'))
- grad_queries: float32 [16384, 8, 128], P(('seq', 'head'))
- grad_prior: float32 [4, 128, 64, 128], P(None, 'head')
The draws below stay inside these ranges and needn't reach their ends.
All inputs are finite; a program needn't handle non-finite values.
Results may differ from the reference program's by a relative error of at most 0.015.
Values may be sent and summed in bfloat16 or wider, within the bound.
A program may use at most 64 MiB of HBM per device.

```python
import jax
import jax.numpy as jnp
from jax import lax

HEADS = 128
HEAD_DIM = 64
STATE = 128
GROUPS = 8
LEVELS = 20
PLEVELS = 4
TOK_DEV = 512
TOKENS = 16384
N_SEQ = 32


def plant(array, rng, smallest, largest):
    place = [jax.random.randint(jax.random.fold_in(rng, axis), (), 0, length) for axis, length in enumerate(array.shape)]
    main_axis = array.shape.index(max(array.shape))
    next_to = place[:main_axis] + [(place[main_axis] + 1) % array.shape[main_axis]] + place[main_axis + 1:]
    return array.at[tuple(place)].set(smallest).at[tuple(next_to)].set(largest)


def block_scale(stream_key, shape, shards, low, largest):
    gain = 1.0
    for dim, shards_of in shards:
        steps = jax.random.uniform(jax.random.fold_in(jax.random.fold_in(stream_key, 6), dim), (shards_of,), jnp.float32, low / len(shards), largest / len(shards))
        gain = gain * jnp.repeat(jnp.exp(steps), shape[dim] // shards_of).reshape((-1,) + (1,) * (len(shape) - 1 - dim))
    return gain


def centred(key, shape, width, bound, split=(), held_as=jnp.bfloat16):
    level = block_scale(key, shape, split, -0.22, 0.18) if split else 1.0
    values = jax.random.normal(key, shape, jnp.float32) * width * level
    return jnp.minimum(jnp.maximum(values, -bound), bound).astype(held_as)


def setup_inputs(seed: int = 0) -> dict:
    streams_of = jax.random.split(jax.random.key(seed), 8)
    return {
        "values": centred(streams_of[0], (TOKENS, HEADS * HEAD_DIM), 1.0, 6.0, ((0, 32), (1, 16))),
        "group_keys": jnp.clip(jax.random.uniform(streams_of[1], (TOKENS, GROUPS, STATE), jnp.float32, -0.5, 0.5) * block_scale(streams_of[1], (TOKENS, GROUPS, STATE), ((0, 512),), -0.4, 0.0), -0.5, 0.5).astype(jnp.bfloat16),
        "group_queries": jnp.clip(jax.random.uniform(streams_of[2], (TOKENS, GROUPS, STATE), jnp.float32, -0.16992188, 0.16992188) * block_scale(streams_of[2], (TOKENS, GROUPS, STATE), ((0, 512),), -0.4, 0.0), -0.16992188, 0.16992188).astype(jnp.bfloat16),
        "level_table": plant(jax.random.randint(streams_of[3], (HEADS, LEVELS), 1, 5), jax.random.fold_in(streams_of[3], 1), 1, 4).astype(jnp.int32),
        "window_index": jax.random.randint(streams_of[4], (1,), 0, 2 ** PLEVELS).astype(jnp.int32),
        "prior_states": jnp.clip(jax.random.uniform(streams_of[5], (PLEVELS, HEADS, HEAD_DIM, STATE), jnp.float32, -100.0, 100.0) * block_scale(streams_of[5], (PLEVELS, HEADS, HEAD_DIM, STATE), ((1, 16),), -0.4, 0.0), -100.0, 100.0).astype(jnp.bfloat16),
        "cotangent": centred(streams_of[6], (TOKENS, HEADS * HEAD_DIM), 0.5, 6.0, ((0, 32), (1, 16))),
    }


def level_weights(level_table):
    level_count = level_table.shape[1]
    exponent = jnp.maximum(jnp.arange(level_count, dtype=jnp.float32) - 1.0, 0.0) * 0.5
    return level_table.astype(jnp.float32) * jnp.exp2(-exponent)


def highest_bit(numbers, bit_count):
    result = jnp.zeros(numbers.shape, jnp.int32)
    for bit_shift in range(1, bit_count):
        result = result + (numbers >= (1 << bit_shift)).astype(jnp.int32)
    return result


def reference(values, group_keys, group_queries, level_table, window_index, prior_states, cotangent):
    highest = lax.Precision.HIGHEST
    log_rows = TOK_DEV.bit_length() - 1
    log_seq = N_SEQ.bit_length() - 1
    log_window = log_rows + log_seq
    per_group = HEADS // GROUPS
    weights = level_weights(level_table)
    value_view = values.reshape(N_SEQ, TOK_DEV, GROUPS, per_group, HEAD_DIM)
    cot_view = cotangent.reshape(N_SEQ, TOK_DEV, GROUPS, per_group, HEAD_DIM)
    key_view = group_keys.reshape(N_SEQ, TOK_DEV, GROUPS, STATE)
    query_view = group_queries.reshape(N_SEQ, TOK_DEV, GROUPS, STATE)

    def segment_states(operands):
        value_seg, key_seg = operands
        outer = jnp.einsum("tgkp,tgn->gkpn", value_seg.astype(jnp.float32), key_seg.astype(jnp.float32), precision=highest)
        return outer.reshape(HEADS, HEAD_DIM, STATE).astype(jnp.bfloat16)

    states = lax.map(segment_states, (value_view, key_view))
    adjoints = lax.map(segment_states, (cot_view, query_view))
    segments = jnp.arange(N_SEQ, dtype=jnp.int32)
    seg_levels = 1 + log_rows + highest_bit(jnp.bitwise_xor(segments[:, None], segments[None, :]), log_seq)
    pair_weights = jnp.where((segments[None, :] < segments[:, None])[None], weights[:, seg_levels], 0.0)
    inflow = jnp.einsum("hij,jhpn->ihpn", pair_weights, states.astype(jnp.float32), precision=highest)
    outflow = jnp.einsum("hij,ihpn->jhpn", pair_weights, adjoints.astype(jnp.float32), precision=highest)
    window_bits = ((window_index[0] >> jnp.arange(PLEVELS, dtype=jnp.int32)) & 1).astype(jnp.float32)
    prior_weights = weights[:, 1 + log_window:1 + log_window + PLEVELS] * window_bits[None, :]
    prior_term = jnp.einsum("hk,khpn->hpn", prior_weights, prior_states.astype(jnp.float32), precision=highest)
    inflow_cast = (inflow + prior_term[None]).astype(jnp.bfloat16)
    outflow_cast = outflow.astype(jnp.bfloat16)
    grand_total = jnp.sum(adjoints.astype(jnp.float32), axis=0)
    grad_prior = prior_weights.T[:, :, None, None] * grand_total[None]

    positions = jnp.arange(TOK_DEV, dtype=jnp.int32)
    spread = jnp.bitwise_xor(positions[:, None], positions[None, :])
    level_grid = jnp.where(spread == 0, 0, 1 + highest_bit(spread, log_rows))
    causal = positions[:, None] >= positions[None, :]
    group_weights = weights.reshape(GROUPS, per_group, LEVELS)
    inflow_groups = inflow_cast.reshape(N_SEQ, GROUPS, per_group, HEAD_DIM, STATE)
    outflow_groups = outflow_cast.reshape(N_SEQ, GROUPS, per_group, HEAD_DIM, STATE)

    def one_group(operands):
        value_grp, cot_grp, key_grp, query_grp, inflow_grp, outflow_grp, weight_grp = operands
        factor_grid = jnp.where(causal[None], weight_grp[:, level_grid], 0.0)
        scores = jnp.dot(query_grp, key_grp.T, preferred_element_type=jnp.float32)
        weighted = (factor_grid * scores[None]).astype(jnp.bfloat16)
        weighted_wide = weighted.astype(jnp.float32)
        value_wide = value_grp.astype(jnp.float32)
        cot_wide = cot_grp.astype(jnp.float32)
        key_wide = key_grp.astype(jnp.float32)
        query_wide = query_grp.astype(jnp.float32)
        inflow_wide = inflow_grp.astype(jnp.float32)
        outflow_wide = outflow_grp.astype(jnp.float32)
        mixer_rows = jnp.einsum("hts,shp->thp", weighted_wide, value_wide, precision=highest)
        mixer_rows = mixer_rows + jnp.einsum("tn,hpn->thp", query_wide, inflow_wide, precision=highest)
        grad_raw = jnp.einsum("thp,shp->hts", cot_wide, value_wide, precision=highest)
        grad_weighted = (factor_grid * grad_raw).astype(jnp.bfloat16).astype(jnp.float32)
        value_grad = jnp.einsum("hts,thp->shp", weighted_wide, cot_wide, precision=highest)
        value_grad = value_grad + jnp.einsum("sn,hpn->shp", key_wide, outflow_wide, precision=highest)
        query_grad = jnp.einsum("hts,sn->tn", grad_weighted, key_wide, precision=highest)
        query_grad = query_grad + jnp.einsum("thp,hpn->tn", cot_wide, inflow_wide, precision=highest)
        key_grad = jnp.einsum("hts,tn->sn", grad_weighted, query_wide, precision=highest)
        key_grad = key_grad + jnp.einsum("shp,hpn->sn", value_wide, outflow_wide, precision=highest)
        return mixer_rows.astype(jnp.bfloat16), value_grad.astype(jnp.bfloat16), query_grad, key_grad

    def one_segment(operands):
        value_seg, cot_seg, key_seg, query_seg, inflow_seg, outflow_seg = operands
        return lax.map(one_group, (jnp.moveaxis(value_seg, 1, 0), jnp.moveaxis(cot_seg, 1, 0), jnp.moveaxis(key_seg, 1, 0), jnp.moveaxis(query_seg, 1, 0), inflow_seg, outflow_seg, group_weights))

    mixer_all, value_all, query_all, key_all = lax.map(one_segment, (value_view, cot_view, key_view, query_view, inflow_groups, outflow_groups))
    mixer_out = jnp.transpose(mixer_all, (0, 2, 1, 3, 4)).reshape(TOKENS, HEADS * HEAD_DIM)
    grad_values = jnp.transpose(value_all, (0, 2, 1, 3, 4)).reshape(TOKENS, HEADS * HEAD_DIM)
    grad_queries = jnp.transpose(query_all, (0, 2, 1, 3)).reshape(TOKENS, GROUPS, STATE)
    grad_keys = jnp.transpose(key_all, (0, 2, 1, 3)).reshape(TOKENS, GROUPS, STATE)
    return mixer_out, grad_values, grad_keys, grad_queries, grad_prior
```

```python
import jax
import jax.numpy as jnp
from jax import lax
from jax.experimental import pallas as pl
from jax.experimental.pallas import tpu as pltpu
from jax.sharding import PartitionSpec as P

HEADS = 128
GROUPS = 8
NS = 32
NH = 16
TOK = 512
HP = 512
LOC = 8
N = 128
BF = jnp.bfloat16
F32 = jnp.float32
MESH = pl.DeviceIdType.MESH

NN = (((1,), (0,)), ((), ()))
NT = (((1,), (1,)), ((), ()))
TN = (((0,), (0,)), ((), ()))


def mm(a, b, dims=NN):
    return lax.dot_general(a, b, dims, preferred_element_type=F32)


def root(level):
    return float(2.0 ** (-max(level - 1, 0) / 2))


def hops():
    rel = [(dy, dx, dc) for dy in range(4) for dx in range(4) for dc in range(2)]
    rel.remove((0, 0, 0))
    near = lambda a: min(a, 4 - a)
    rel.sort(key=lambda r: -(near(r[0]) + near(r[1])))
    return rel


def kernel(
    v_hbm, k_hbm, q_hbm, table, window, prior_hbm, c_hbm,
    mix_hbm, gv_hbm, gk_hbm, gq_hbm, tot_hbm, prior_w_hbm,
    v, c, kraw, qraw, prior, vt, ct, kq_send, kq, factor, factor_t,
    g_diag, g_8, g_9, sa_send, sa_recv, io_send, io_recv, tot_send, tot_recv,
    mix, gval, grad, mate_send, mate_recv, out_send, back, outs, rows_out, prior_w,
    local_sem, gat_send, gat_recv, fwd_send, sa_ss, sa_rs, io_ss, io_rs, tot_ss, tot_rs,
    mt_ss, mt_rs, bk_ss, bk_rs,
):
    me = lax.axis_index("seq")
    z = lax.axis_index("head")
    pair = lax.div(z, 2)
    odd = lax.rem(z, 2)
    sgn = 2 * odd - 1
    mate = z - sgn
    ring = lambda i: lax.rem(i + 2 * NH, NH)
    core, xx, yy = lax.rem(me, 2), lax.rem(lax.div(me, 2), 4), lax.div(me, 8)

    def seq_of(rel):
        dy, dx, dc = rel
        return lax.rem(yy + dy, 4) * 8 + lax.rem(xx + dx, 4) * 2 + lax.rem(core + dc, 2)

    relative = hops()
    near_z = [ring(z + sgn * j) for j in range(1, 8)]
    far_z = [ring(z - sgn * j) for j in (2, 4, 6)]

    loads = [
        pltpu.make_async_copy(k_hbm, kraw, local_sem.at[0]),
        pltpu.make_async_copy(q_hbm, qraw, local_sem.at[1]),
        pltpu.make_async_copy(v_hbm, v, local_sem.at[2]),
        pltpu.make_async_copy(c_hbm, c, local_sem.at[3]),
        pltpu.make_async_copy(prior_hbm.at[:, pl.ds(pl.multiple_of(me * 16, 16), 16), :], prior, local_sem.at[4]),
    ]
    for load in loads:
        load.start()

    barrier = pltpu.get_barrier_semaphore()
    for other in near_z + far_z + [mate]:
        pl.semaphore_signal(barrier, inc=1, device_id={"head": other}, device_id_type=MESH)
    for rel in relative:
        pl.semaphore_signal(barrier, inc=1, device_id={"seq": seq_of(rel)}, device_id_type=MESH)

    out_row = lax.broadcasted_iota(jnp.int32, (256, 256), 0)
    in_row = lax.broadcasted_iota(jnp.int32, (256, 256), 1)
    pick = (in_row == (out_row & 31) * 8 + (out_row >> 5)).astype(F32).astype(BF)
    loads[0].wait()
    k_sorted = mm(pick, kraw[...]).astype(BF)
    loads[1].wait()
    q_sorted = mm(pick, qraw[...]).astype(BF)
    for g in range(GROUPS):
        kq_send[g, 0:32, :] = k_sorted[32 * g : 32 * g + 32, :]
        kq_send[g, 32:64, :] = q_sorted[32 * g : 32 * g + 32, :]
    kq[z] = kq_send[pair]

    weight = lambda h, l: table[h, l].astype(F32) * root(l)
    row = lax.broadcasted_iota(jnp.int32, (128, 128), 0)
    col = lax.broadcasted_iota(jnp.int32, (128, 128), 1)
    spread = row ^ col
    for h in range(LOC):
        grid = jnp.full((128, 128), weight(h, 7), F32)
        for l in range(6, -1, -1):
            grid = jnp.where(spread < (1 << l), weight(h, l), grid)
        factor[h] = jnp.where(row >= col, grid, 0.0)
        factor_t[h] = jnp.where(col >= row, grid, 0.0)

    lane = lax.broadcasted_iota(jnp.int32, (1, HP), 1) >> 6

    def lanes_of(level):
        w = jnp.zeros((1, HP), F32)
        for h in range(LOC):
            w = jnp.where(lane == h, weight(h, level), w)
        return w

    w8, w9 = lanes_of(8), lanes_of(9)
    low_half = lax.broadcasted_iota(jnp.int32, (128, 128), 1) < 64

    def both(ref, i, pr):
        tile = ref[128 * i : 128 * i + 128, 128 * pr : 128 * pr + 128]
        zero = jnp.zeros_like(tile)
        return jnp.concatenate([jnp.where(low_half, tile, zero), jnp.where(low_half, zero, tile)], axis=0)

    loads[2].wait()
    loads[3].wait()
    vt[...] = v[...].T
    ct[...] = c[...].T

    def wide_grads():
        g_9[...] = mm((c[256:512, :].astype(F32) * w9).astype(BF), v[0:256, :], NT).astype(BF)
        for i in range(2):
            at = 256 * i
            g_8[i] = mm((c[at + 128 : at + 256, :].astype(F32) * w8).astype(BF), v[at : at + 128, :], NT).astype(BF)

    def diagonal_grads(i):
        total = jnp.zeros((128, 128), F32)
        for pr in range(4):
            raw = mm(both(c, i, pr), v[128 * i : 128 * i + 128, 128 * pr : 128 * pr + 128], NT)
            total = total + factor[2 * pr] * raw[:128] + factor[2 * pr + 1] * raw[128:]
        g_diag[i] = total.astype(BF)

    pl.semaphore_wait(barrier, 11 + 31)

    def gather_copy(block, to):
        return pltpu.make_async_remote_copy(
            src_ref=kq_send.at[block], dst_ref=kq.at[z], send_sem=gat_send.at[block], recv_sem=gat_recv.at[z],
            device_id={"head": to}, device_id_type=MESH,
        )

    opposite = lax.rem(pair + 4, 8)
    gathers = [gather_copy(opposite, 2 * opposite + 1 - odd)]
    for k in (3, 2, 1):
        right, left = lax.rem(pair + k, 8), lax.rem(pair + 8 - k, 8)
        gathers += [gather_copy(right, 2 * right), gather_copy(left, 2 * left + 1)]
    gathers.append(gather_copy(pair, mate))
    for copy in gathers:
        copy.start()

    wide_grads()
    for i in range(4):
        diagonal_grads(i)

    forwards = []
    for j in range(7):
        src = near_z[j]
        pltpu.make_async_remote_copy(
            src_ref=kq.at[src], dst_ref=kq.at[src], send_sem=gat_send.at[0], recv_sem=gat_recv.at[src],
            device_id={"head": mate}, device_id_type=MESH,
        ).wait_recv()
        forward = pltpu.make_async_remote_copy(
            src_ref=kq.at[src], dst_ref=kq.at[src], send_sem=fwd_send.at[j], recv_sem=gat_recv.at[src],
            device_id={"head": mate}, device_id_type=MESH,
        )
        forward.start()
        forwards.append(forward)
    for src in [mate] + [ring(mate - sgn * j) for j in range(1, 8)]:
        pltpu.make_async_remote_copy(
            src_ref=kq.at[src], dst_ref=kq.at[src], send_sem=gat_send.at[0], recv_sem=gat_recv.at[src],
            device_id={"head": mate}, device_id_type=MESH,
        ).wait_recv()

    keys = kq[:, 0:32, :].reshape(TOK, N)
    queries = kq[:, 32:64, :].reshape(TOK, N)

    sa_send[:, 0] = mm(vt[...], keys).astype(BF).reshape(NS, 16, N)
    sa_send[:, 1] = mm(ct[...], queries).astype(BF).reshape(NS, 16, N)

    def spread_out(src, dst, ss, rs, whole):
        copies = []
        for n, rel in enumerate(relative):
            to = seq_of(rel)
            copies.append(pltpu.make_async_remote_copy(
                src_ref=src if whole else src.at[to], dst_ref=dst.at[me], send_sem=ss.at[n], recv_sem=rs.at[me],
                device_id={"seq": to}, device_id_type=MESH,
            ))
        for copy in copies:
            copy.start()
        return copies

    def arrive(dst, ss, rs):
        for rel in relative:
            frm = seq_of(rel)
            pltpu.make_async_remote_copy(
                src_ref=dst.at[frm], dst_ref=dst.at[frm], send_sem=ss.at[0], recv_sem=rs.at[frm],
                device_id={"seq": frm}, device_id_type=MESH,
            ).wait_recv()

    sa_copies = spread_out(sa_send, sa_recv, sa_ss, sa_rs, False)
    sa_recv[me] = sa_send[me]

    def block(i):
        return slice(128 * i, 128 * i + 128)

    def inner_outputs():
        for i in range(4):
            q_i, k_i = queries[block(i)], keys[block(i)]
            score, score_t = mm(q_i, k_i, NT), mm(k_i, q_i, NT)
            for pr in range(4):
                cols = slice(128 * pr, 128 * pr + 128)
                w = jnp.concatenate([(factor[2 * pr] * score).astype(BF), (factor[2 * pr + 1] * score).astype(BF)], axis=1)
                mix[block(i), cols] = mm(w, both(v, i, pr))
                w = jnp.concatenate([(factor_t[2 * pr] * score_t).astype(BF), (factor_t[2 * pr + 1] * score_t).astype(BF)], axis=1)
                gval[block(i), cols] = mm(w, both(c, i, pr))
        for i in range(2):
            lo, hi = block(2 * i), block(2 * i + 1)
            mix[hi, :] += w8 * mm(mm(queries[hi], keys[lo], NT).astype(BF), v[lo, :])
            gval[lo, :] += w8 * mm(mm(keys[lo], queries[hi], NT).astype(BF), c[hi, :])
        lo, hi = slice(0, 256), slice(256, 512)
        mix[hi, :] += w9 * mm(mm(queries[hi], keys[lo], NT).astype(BF), v[lo, :])
        gval[lo, :] += w9 * mm(mm(keys[lo], queries[hi], NT).astype(BF), c[hi, :])

    def inner_grads():
        for i in range(4):
            gq = mm(g_diag[i], keys[block(i)])
            gk = mm(g_diag[i], queries[block(i)], TN)
            if i % 2 == 1:
                gq = gq + mm(g_8[i // 2], keys[block(i - 1)])
            else:
                gk = gk + mm(g_8[i // 2], queries[block(i + 1)], TN)
            if i >= 2:
                gq = gq + mm(g_9[128 * (i - 2) : 128 * (i - 1), :], keys[0:256])
            else:
                gk = gk + mm(g_9[:, 128 * i : 128 * (i + 1)], queries[256:512], TN)
            grad[4 * i : 4 * i + 4, 0:32] = gk.reshape(4, 32, N)
            grad[4 * i : 4 * i + 4, 32:64] = gq.reshape(4, 32, N)

    inner_grads()

    arrive(sa_recv, sa_ss, sa_rs)
    my_head = lax.div(me, 4)
    seq_w = [table[my_head, 10 + b].astype(F32) * root(10 + b) for b in range(5)]
    bit = lambda k: ((window[0] >> k) & 1).astype(F32)
    loads[4].wait()
    start = jnp.zeros((16, N), F32)
    for k in range(4):
        start = start + (table[my_head, 15 + k].astype(F32) * root(15 + k) * bit(k)) * prior[k].astype(F32)

    def sums(which):
        levels = [[sa_recv[j, which].astype(F32) for j in range(NS)]]
        for _ in range(5):
            last = levels[-1]
            levels.append([last[2 * j] + last[2 * j + 1] for j in range(len(last) // 2)])
        return levels

    levels = sums(0)
    flow = [start]
    for b in range(4, -1, -1):
        flow = [x for j, f in enumerate(flow) for x in (f, f + seq_w[b] * levels[b][2 * j])]
    for j in range(NS):
        io_send[j, 0] = flow[j].astype(BF)
    levels = sums(1)
    flow = [jnp.zeros((16, N), F32)]
    for b in range(4, -1, -1):
        flow = [x for j, f in enumerate(flow) for x in (f + seq_w[b] * levels[b][2 * j + 1], f)]
    for j in range(NS):
        io_send[j, 1] = flow[j].astype(BF)
    tot_send[...] = levels[5][0].astype(BF)

    io_copies = spread_out(io_send, io_recv, io_ss, io_rs, False)
    tot_copies = spread_out(tot_send, tot_recv, tot_ss, tot_rs, True)
    io_recv[me] = io_send[me]
    tot_recv[me] = tot_send[...]

    inner_outputs()

    arrive(io_recv, io_ss, io_rs)
    inflow = io_recv[:, 0].reshape(HP, N)
    outflow = io_recv[:, 1].reshape(HP, N)
    grad[:, 0:32] = grad[:, 0:32] + mm(v[...], outflow).reshape(NH, 32, N)
    grad[:, 32:64] = grad[:, 32:64] + mm(c[...], inflow).reshape(NH, 32, N)
    mate_send[...] = grad[...].astype(BF)

    mate_copies = []
    for j in range(7, -1, -1):
        rows = ring(mate - sgn * j)
        mate_copies.append(pltpu.make_async_remote_copy(
            src_ref=mate_send.at[rows], dst_ref=mate_recv.at[j], send_sem=mt_ss.at[j], recv_sem=mt_rs.at[j],
            device_id={"head": mate}, device_id_type=MESH,
        ))
    for copy in mate_copies:
        copy.start()

    def mate_arrive(j):
        pltpu.make_async_remote_copy(
            src_ref=mate_recv.at[j], dst_ref=mate_recv.at[j], send_sem=mt_ss.at[j], recv_sem=mt_rs.at[j],
            device_id={"head": mate}, device_id_type=MESH,
        ).wait_recv()

    back_copies = []
    for j in range(7, 0, -1):
        to = near_z[j - 1]
        mate_arrive(j)
        out_send[j] = (grad[to] + mate_recv[j].astype(F32)).astype(BF)
        copy = pltpu.make_async_remote_copy(
            src_ref=out_send.at[j], dst_ref=back.at[pair], send_sem=bk_ss.at[j], recv_sem=bk_rs.at[pair],
            device_id={"head": to}, device_id_type=MESH,
        )
        copy.start()
        back_copies.append(copy)
    mate_arrive(0)
    back[pair] = (grad[z] + mate_recv[0].astype(F32)).astype(BF)

    stores = []

    def store(src, dst):
        stores.append(pltpu.make_async_copy(src, dst, local_sem.at[5 + len(stores)]))
        stores[-1].start()

    outs[0] = (mix[...] + mm(queries, inflow, NT)).astype(BF)
    store(outs.at[0], mix_hbm)
    outs[1] = (gval[...] + mm(keys, outflow, NT)).astype(BF)
    store(outs.at[1], gv_hbm)
    for h in range(LOC):
        for k in range(4):
            prior_w[8 * k + h : 8 * k + h + 1, :] = jnp.full((1, N), weight(h, 15 + k) * bit(k), F32)
    store(prior_w, prior_w_hbm)
    arrive(tot_recv, tot_ss, tot_rs)
    store(tot_recv, tot_hbm)

    for k in range(1, 8):
        frm = lax.rem(pair + k, 8)
        pltpu.make_async_remote_copy(
            src_ref=back.at[frm], dst_ref=back.at[frm], send_sem=bk_ss.at[0], recv_sem=bk_rs.at[frm],
            device_id={"head": mate}, device_id_type=MESH,
        ).wait_recv()
    for g in range(GROUPS):
        rows_out[0, pl.ds(g, 32, stride=8), :] = back[g, 0:32].astype(F32)
        rows_out[1, pl.ds(g, 32, stride=8), :] = back[g, 32:64].astype(F32)
    store(rows_out.at[0], gk_hbm)
    store(rows_out.at[1], gq_hbm)

    for copy in gathers + forwards + sa_copies + io_copies + tot_copies + mate_copies + back_copies:
        copy.wait_send()
    for copy in stores:
        copy.wait()


def store_kernel(*refs):
    ins, outs, held, sems = refs[:6], refs[6:11], refs[11:18], refs[18]
    order = (4, 5, 0, 1, 2, 3)
    loads = [pltpu.make_async_copy(ins[i], held[i], sems.at[i]) for i in range(6)]
    for i in order:
        loads[i].start()
    loads[4].wait()
    loads[5].wait()
    tot, prior_w, gp = held[4], held[5], held[6]
    stores = []
    for k in range(4):
        for h in range(LOC):
            piece = tot[4 * h : 4 * h + 4].reshape(64, N).astype(F32)
            gp[k, 64 * h : 64 * h + 64, :] = prior_w[8 * k + h : 8 * k + h + 1, :] * piece
        stores.append(pltpu.make_async_copy(gp.at[k], outs[4].at[k], sems.at[6 + k]))
        stores[-1].start()
    for i in range(4):
        loads[i].wait()
        stores.append(pltpu.make_async_copy(held[i], outs[i], sems.at[10 + i]))
        stores[-1].start()
    for copy in stores:
        copy.wait()


def per_device(values, group_keys, group_queries, level_table, window_index, prior_states, cotangent):
    hbm = pl.BlockSpec(memory_space=pltpu.HBM)
    smem = pl.BlockSpec(memory_space=pltpu.SMEM)
    dma = pltpu.SemaphoreType.DMA
    wide, narrow = jax.ShapeDtypeStruct((TOK, HP), BF), jax.ShapeDtypeStruct((256, N), F32)
    parts = pl.pallas_call(
        kernel,
        out_shape=(
            wide, wide, narrow, narrow,
            jax.ShapeDtypeStruct((NS, 16, N), BF),
            jax.ShapeDtypeStruct((32, N), F32),
        ),
        in_specs=[hbm, hbm, hbm, smem, smem, hbm, hbm],
        out_specs=(hbm,) * 6,
        scratch_shapes=[
            pltpu.VMEM((TOK, HP), BF),
            pltpu.VMEM((TOK, HP), BF),
            pltpu.VMEM((256, N), BF),
            pltpu.VMEM((256, N), BF),
            pltpu.VMEM((4, 16, N), BF),
            pltpu.VMEM((HP, TOK), BF),
            pltpu.VMEM((HP, TOK), BF),
            pltpu.VMEM((GROUPS, 64, N), BF),
            pltpu.VMEM((NH, 64, N), BF),
            pltpu.VMEM((LOC, 128, 128), F32),
            pltpu.VMEM((LOC, 128, 128), F32),
            pltpu.VMEM((4, 128, 128), BF),
            pltpu.VMEM((2, 128, 128), BF),
            pltpu.VMEM((256, 256), BF),
            pltpu.VMEM((NS, 2, 16, N), BF),
            pltpu.VMEM((NS, 2, 16, N), BF),
            pltpu.VMEM((NS, 2, 16, N), BF),
            pltpu.VMEM((NS, 2, 16, N), BF),
            pltpu.VMEM((16, N), BF),
            pltpu.VMEM((NS, 16, N), BF),
            pltpu.VMEM((TOK, HP), F32),
            pltpu.VMEM((TOK, HP), F32),
            pltpu.VMEM((NH, 64, N), F32),
            pltpu.VMEM((NH, 64, N), BF),
            pltpu.VMEM((8, 64, N), BF),
            pltpu.VMEM((8, 64, N), BF),
            pltpu.VMEM((GROUPS, 64, N), BF),
            pltpu.VMEM((2, TOK, HP), BF),
            pltpu.VMEM((2, 256, N), F32),
            pltpu.VMEM((32, N), F32),
            dma((11,)),
            dma((GROUPS,)),
            dma((NH,)),
            dma((7,)),
            dma((NS,)),
            dma((NS,)),
            dma((NS,)),
            dma((NS,)),
            dma((NS,)),
            dma((NS,)),
            dma((8,)),
            dma((8,)),
            dma((8,)),
            dma((8,)),
        ],
        compiler_params=pltpu.CompilerParams(
            collective_id=0, has_side_effects=True, vmem_limit_bytes=62 * 1024 * 1024
        ),
    )(
        values,
        group_keys.reshape(256, N),
        group_queries.reshape(256, N),
        level_table,
        window_index,
        prior_states.reshape(4, HP, N),
        cotangent,
    )
    outs = pl.pallas_call(
        store_kernel,
        out_shape=(wide, wide, narrow, narrow, jax.ShapeDtypeStruct((4, HP, N), F32)),
        in_specs=[hbm] * 6,
        out_specs=(hbm,) * 5,
        scratch_shapes=[
            pltpu.VMEM((TOK, HP), BF),
            pltpu.VMEM((TOK, HP), BF),
            pltpu.VMEM((256, N), F32),
            pltpu.VMEM((256, N), F32),
            pltpu.VMEM((NS, 16, N), BF),
            pltpu.VMEM((32, N), F32),
            pltpu.VMEM((4, HP, N), F32),
            dma((14,)),
        ],
        compiler_params=pltpu.CompilerParams(vmem_limit_bytes=62 * 1024 * 1024),
    )(*parts)
    mixer_out, grad_values, grad_keys, grad_queries, grad_prior = outs
    return (
        mixer_out,
        grad_values,
        grad_keys.reshape(32, GROUPS, N),
        grad_queries.reshape(32, GROUPS, N),
        grad_prior.reshape(4, LOC, 64, N),
    )


def solution(mesh):
    rows = P(("seq", "head"), None, None)
    return jax.shard_map(
        per_device,
        mesh=mesh,
        in_specs=(P("seq", "head"), rows, rows, P("head", None), P(), P(None, "head", None, None), P("seq", "head")),
        out_specs=(P("seq", "head"), P("seq", "head"), rows, rows, P(None, "head", None, None)),
        check_vma=False,
    )
```

```python
import jax
import jax.numpy as jnp
from jax import lax
from jax.experimental import pallas as pl
from jax.experimental.pallas import tpu as pltpu
from jax.sharding import PartitionSpec as P

HEADS = 128
GROUPS = 8
NS = 32
NH = 16
TOK = 512
HP = 512
LOC = 8
N = 128
BF = jnp.bfloat16
F32 = jnp.float32
MESH = pl.DeviceIdType.MESH

NN = (((1,), (0,)), ((), ()))
NT = (((1,), (1,)), ((), ()))
TN = (((0,), (0,)), ((), ()))


def mm(a, b, dims=NN):
    return lax.dot_general(a, b, dims, preferred_element_type=F32)


def root(level):
    return float(2.0 ** (-max(level - 1, 0) / 2))


def hops():
    rel = [(dy, dx, dc) for dy in range(4) for dx in range(4) for dc in range(2)]
    rel.remove((0, 0, 0))
    near = lambda a: min(a, 4 - a)
    rel.sort(key=lambda r: -(near(r[0]) + near(r[1])))
    return rel


def kernel(
    v_hbm, k_hbm, q_hbm, table_hbm, window_hbm, prior_hbm, c_hbm,
    mix_hbm, gv_hbm, gk_hbm, gq_hbm, tot_hbm, prior_w_hbm,
    table, window, v, c, kraw, qraw, prior, vt, ct, kq_send, kq, factor, factor_t,
    g_diag, g_8, g_9, sa_send, sa_recv, io_send, io_recv, tot_send, tot_recv,
    mix, gval, grad, mate_send, mate_recv, out_send, back, outs, rows_out, prior_w,
    local_sem, gat_send, gat_recv, fwd_send, sa_ss, sa_rs, io_ss, io_rs, tot_ss, tot_rs,
    mt_ss, mt_rs, bk_ss, bk_rs,
):
    me = lax.axis_index("seq")
    z = lax.axis_index("head")
    pair = lax.div(z, 2)
    odd = lax.rem(z, 2)
    sgn = 2 * odd - 1
    mate = z - sgn
    ring = lambda i: lax.rem(i + 2 * NH, NH)
    core, xx, yy = lax.rem(me, 2), lax.rem(lax.div(me, 2), 4), lax.div(me, 8)

    def seq_of(rel):
        dy, dx, dc = rel
        return lax.rem(yy + dy, 4) * 8 + lax.rem(xx + dx, 4) * 2 + lax.rem(core + dc, 2)

    relative = hops()
    near_z = [ring(z + sgn * j) for j in range(1, 8)]
    far_z = [ring(z - sgn * j) for j in (2, 4, 6)]

    barrier = pltpu.get_barrier_semaphore()
    for other in near_z + far_z + [mate]:
        pl.semaphore_signal(barrier, inc=1, device_id={"head": other}, device_id_type=MESH)
    for rel in relative:
        pl.semaphore_signal(barrier, inc=1, device_id={"seq": seq_of(rel)}, device_id_type=MESH)

    loads = [
        pltpu.make_async_copy(k_hbm, kraw, local_sem.at[0]),
        pltpu.make_async_copy(q_hbm, qraw, local_sem.at[1]),
        pltpu.make_async_copy(v_hbm, v, local_sem.at[2]),
        pltpu.make_async_copy(c_hbm, c, local_sem.at[3]),
        pltpu.make_async_copy(prior_hbm.at[:, pl.ds(pl.multiple_of(me * 16, 16), 16), :], prior, local_sem.at[4]),
        pltpu.make_async_copy(table_hbm, table, local_sem.at[11]),
        pltpu.make_async_copy(window_hbm, window, local_sem.at[12]),
    ]
    for load in loads:
        load.start()

    out_row = lax.broadcasted_iota(jnp.int32, (256, 256), 0)
    in_row = lax.broadcasted_iota(jnp.int32, (256, 256), 1)
    pick = (in_row == (out_row & 31) * 8 + (out_row >> 5)).astype(F32).astype(BF)
    loads[0].wait()
    k_sorted = mm(pick, kraw[...]).astype(BF)
    loads[1].wait()
    q_sorted = mm(pick, qraw[...]).astype(BF)
    for g in range(GROUPS):
        kq_send[g, 0:32, :] = k_sorted[32 * g : 32 * g + 32, :]
        kq_send[g, 32:64, :] = q_sorted[32 * g : 32 * g + 32, :]
    kq[z] = kq_send[pair]

    loads[5].wait()
    weight = lambda h, l: table[h, l].astype(F32) * root(l)
    row = lax.broadcasted_iota(jnp.int32, (128, 128), 0)
    col = lax.broadcasted_iota(jnp.int32, (128, 128), 1)
    spread = row ^ col
    for h in range(LOC):
        grid = jnp.full((128, 128), weight(h, 7), F32)
        for l in range(6, -1, -1):
            grid = jnp.where(spread < (1 << l), weight(h, l), grid)
        factor[h] = jnp.where(row >= col, grid, 0.0)
        factor_t[h] = jnp.where(col >= row, grid, 0.0)

    lane = lax.broadcasted_iota(jnp.int32, (1, HP), 1) >> 6

    def lanes_of(level):
        w = jnp.zeros((1, HP), F32)
        for h in range(LOC):
            w = jnp.where(lane == h, weight(h, level), w)
        return w

    w8, w9 = lanes_of(8), lanes_of(9)
    low_half = lax.broadcasted_iota(jnp.int32, (128, 128), 1) < 64

    def both(ref, i, pr):
        tile = ref[128 * i : 128 * i + 128, 128 * pr : 128 * pr + 128]
        zero = jnp.zeros_like(tile)
        return jnp.concatenate([jnp.where(low_half, tile, zero), jnp.where(low_half, zero, tile)], axis=0)

    loads[2].wait()
    loads[3].wait()
    vt[...] = v[...].T
    ct[...] = c[...].T

    def wide_grads():
        g_9[...] = mm((c[256:512, :].astype(F32) * w9).astype(BF), v[0:256, :], NT).astype(BF)
        for i in range(2):
            at = 256 * i
            g_8[i] = mm((c[at + 128 : at + 256, :].astype(F32) * w8).astype(BF), v[at : at + 128, :], NT).astype(BF)

    def diagonal_grads(i):
        total = jnp.zeros((128, 128), F32)
        for pr in range(4):
            raw = mm(both(c, i, pr), v[128 * i : 128 * i + 128, 128 * pr : 128 * pr + 128], NT)
            total = total + factor[2 * pr] * raw[:128] + factor[2 * pr + 1] * raw[128:]
        g_diag[i] = total.astype(BF)

    pl.semaphore_wait(barrier, 11 + 31)

    def gather_copy(block, to):
        return pltpu.make_async_remote_copy(
            src_ref=kq_send.at[block], dst_ref=kq.at[z], send_sem=gat_send.at[block], recv_sem=gat_recv.at[z],
            device_id={"head": to}, device_id_type=MESH,
        )

    opposite = lax.rem(pair + 4, 8)
    gathers = [gather_copy(opposite, 2 * opposite + 1 - odd)]
    for k in (3, 2, 1):
        right, left = lax.rem(pair + k, 8), lax.rem(pair + 8 - k, 8)
        gathers += [gather_copy(right, 2 * right), gather_copy(left, 2 * left + 1)]
    gathers.append(gather_copy(pair, mate))
    for copy in gathers:
        copy.start()

    wide_grads()
    for i in range(4):
        diagonal_grads(i)

    forwards = []
    for j in range(7):
        src = near_z[j]
        pltpu.make_async_remote_copy(
            src_ref=kq.at[src], dst_ref=kq.at[src], send_sem=gat_send.at[0], recv_sem=gat_recv.at[src],
            device_id={"head": mate}, device_id_type=MESH,
        ).wait_recv()
        forward = pltpu.make_async_remote_copy(
            src_ref=kq.at[src], dst_ref=kq.at[src], send_sem=fwd_send.at[j], recv_sem=gat_recv.at[src],
            device_id={"head": mate}, device_id_type=MESH,
        )
        forward.start()
        forwards.append(forward)
    for src in [mate] + [ring(mate - sgn * j) for j in range(1, 8)]:
        pltpu.make_async_remote_copy(
            src_ref=kq.at[src], dst_ref=kq.at[src], send_sem=gat_send.at[0], recv_sem=gat_recv.at[src],
            device_id={"head": mate}, device_id_type=MESH,
        ).wait_recv()

    keys = kq[:, 0:32, :].reshape(TOK, N)
    queries = kq[:, 32:64, :].reshape(TOK, N)

    sa_send[:, 0] = mm(vt[...], keys).astype(BF).reshape(NS, 16, N)
    sa_send[:, 1] = mm(ct[...], queries).astype(BF).reshape(NS, 16, N)

    def spread_out(src, dst, ss, rs, whole):
        copies = []
        for n, rel in enumerate(relative):
            to = seq_of(rel)
            copies.append(pltpu.make_async_remote_copy(
                src_ref=src if whole else src.at[to], dst_ref=dst.at[me], send_sem=ss.at[n], recv_sem=rs.at[me],
                device_id={"seq": to}, device_id_type=MESH,
            ))
        for copy in copies:
            copy.start()
        return copies

    def arrive(dst, ss, rs):
        for rel in relative:
            frm = seq_of(rel)
            pltpu.make_async_remote_copy(
                src_ref=dst.at[frm], dst_ref=dst.at[frm], send_sem=ss.at[0], recv_sem=rs.at[frm],
                device_id={"seq": frm}, device_id_type=MESH,
            ).wait_recv()

    sa_copies = spread_out(sa_send, sa_recv, sa_ss, sa_rs, False)
    sa_recv[me] = sa_send[me]

    def block(i):
        return slice(128 * i, 128 * i + 128)

    def inner_outputs():
        for i in range(4):
            q_i, k_i = queries[block(i)], keys[block(i)]
            score, score_t = mm(q_i, k_i, NT), mm(k_i, q_i, NT)
            for pr in range(4):
                cols = slice(128 * pr, 128 * pr + 128)
                w = jnp.concatenate([(factor[2 * pr] * score).astype(BF), (factor[2 * pr + 1] * score).astype(BF)], axis=1)
                mix[block(i), cols] = mm(w, both(v, i, pr))
                w = jnp.concatenate([(factor_t[2 * pr] * score_t).astype(BF), (factor_t[2 * pr + 1] * score_t).astype(BF)], axis=1)
                gval[block(i), cols] = mm(w, both(c, i, pr))
        for i in range(2):
            lo, hi = block(2 * i), block(2 * i + 1)
            mix[hi, :] += w8 * mm(mm(queries[hi], keys[lo], NT).astype(BF), v[lo, :])
            gval[lo, :] += w8 * mm(mm(keys[lo], queries[hi], NT).astype(BF), c[hi, :])
        lo, hi = slice(0, 256), slice(256, 512)
        mix[hi, :] += w9 * mm(mm(queries[hi], keys[lo], NT).astype(BF), v[lo, :])
        gval[lo, :] += w9 * mm(mm(keys[lo], queries[hi], NT).astype(BF), c[hi, :])

    def inner_grads():
        for i in range(4):
            gq = mm(g_diag[i], keys[block(i)])
            gk = mm(g_diag[i], queries[block(i)], TN)
            if i % 2 == 1:
                gq = gq + mm(g_8[i // 2], keys[block(i - 1)])
            else:
                gk = gk + mm(g_8[i // 2], queries[block(i + 1)], TN)
            if i >= 2:
                gq = gq + mm(g_9[128 * (i - 2) : 128 * (i - 1), :], keys[0:256])
            else:
                gk = gk + mm(g_9[:, 128 * i : 128 * (i + 1)], queries[256:512], TN)
            grad[4 * i : 4 * i + 4, 0:32] = gk.reshape(4, 32, N)
            grad[4 * i : 4 * i + 4, 32:64] = gq.reshape(4, 32, N)

    inner_grads()

    arrive(sa_recv, sa_ss, sa_rs)
    my_head = lax.div(me, 4)
    seq_w = [table[my_head, 10 + b].astype(F32) * root(10 + b) for b in range(5)]
    bit = lambda k: ((window[0] >> k) & 1).astype(F32)
    loads[4].wait()
    loads[6].wait()
    start = jnp.zeros((16, N), F32)
    for k in range(4):
        start = start + (table[my_head, 15 + k].astype(F32) * root(15 + k) * bit(k)) * prior[k].astype(F32)

    def sums(which):
        levels = [[sa_recv[j, which].astype(F32) for j in range(NS)]]
        for _ in range(5):
            last = levels[-1]
            levels.append([last[2 * j] + last[2 * j + 1] for j in range(len(last) // 2)])
        return levels

    levels = sums(0)
    flow = [start]
    for b in range(4, -1, -1):
        flow = [x for j, f in enumerate(flow) for x in (f, f + seq_w[b] * levels[b][2 * j])]
    for j in range(NS):
        io_send[j, 0] = flow[j].astype(BF)
    levels = sums(1)
    flow = [jnp.zeros((16, N), F32)]
    for b in range(4, -1, -1):
        flow = [x for j, f in enumerate(flow) for x in (f + seq_w[b] * levels[b][2 * j + 1], f)]
    for j in range(NS):
        io_send[j, 1] = flow[j].astype(BF)
    tot_send[...] = levels[5][0].astype(BF)

    io_copies = spread_out(io_send, io_recv, io_ss, io_rs, False)
    tot_copies = spread_out(tot_send, tot_recv, tot_ss, tot_rs, True)
    io_recv[me] = io_send[me]
    tot_recv[me] = tot_send[...]

    inner_outputs()

    arrive(io_recv, io_ss, io_rs)
    inflow = io_recv[:, 0].reshape(HP, N)
    outflow = io_recv[:, 1].reshape(HP, N)
    grad[:, 0:32] = grad[:, 0:32] + mm(v[...], outflow).reshape(NH, 32, N)
    grad[:, 32:64] = grad[:, 32:64] + mm(c[...], inflow).reshape(NH, 32, N)
    mate_send[...] = grad[...].astype(BF)

    def owners(first):
        turn = lax.div(first + 6, NH) * (NH - first)
        return [ring(first + lax.rem(turn + i, 7)) for i in range(7)]

    mine = owners(ring(z - 7 * (1 - odd) + odd))
    mates = owners(ring(mate - 7 * odd + (1 - odd))) + [mate]
    mate_copies = []
    for j in range(8):
        mate_copies.append(pltpu.make_async_remote_copy(
            src_ref=mate_send.at[mates[j]], dst_ref=mate_recv.at[j], send_sem=mt_ss.at[j], recv_sem=mt_rs.at[j],
            device_id={"head": mate}, device_id_type=MESH,
        ))
    for copy in mate_copies:
        copy.start()

    def mate_arrive(j):
        pltpu.make_async_remote_copy(
            src_ref=mate_recv.at[j], dst_ref=mate_recv.at[j], send_sem=mt_ss.at[j], recv_sem=mt_rs.at[j],
            device_id={"head": mate}, device_id_type=MESH,
        ).wait_recv()

    back_copies = []
    for j in range(7):
        to = mine[j]
        mate_arrive(j)
        out_send[j] = (grad[to] + mate_recv[j].astype(F32)).astype(BF)
        copy = pltpu.make_async_remote_copy(
            src_ref=out_send.at[j], dst_ref=back.at[pair], send_sem=bk_ss.at[j], recv_sem=bk_rs.at[pair],
            device_id={"head": to}, device_id_type=MESH,
        )
        copy.start()
        back_copies.append(copy)
    mate_arrive(7)
    back[pair] = (grad[z] + mate_recv[7].astype(F32)).astype(BF)

    stores = []

    def store(src, dst):
        stores.append(pltpu.make_async_copy(src, dst, local_sem.at[5 + len(stores)]))
        stores[-1].start()

    outs[0] = (mix[...] + mm(queries, inflow, NT)).astype(BF)
    store(outs.at[0], mix_hbm)
    outs[1] = (gval[...] + mm(keys, outflow, NT)).astype(BF)
    store(outs.at[1], gv_hbm)
    for h in range(LOC):
        for k in range(4):
            prior_w[8 * k + h : 8 * k + h + 1, :] = jnp.full((1, N), weight(h, 15 + k) * bit(k), F32)
    store(prior_w, prior_w_hbm)
    arrive(tot_recv, tot_ss, tot_rs)
    store(tot_recv, tot_hbm)

    for k in range(1, 8):
        frm = lax.rem(pair + k, 8)
        pltpu.make_async_remote_copy(
            src_ref=back.at[frm], dst_ref=back.at[frm], send_sem=bk_ss.at[0], recv_sem=bk_rs.at[frm],
            device_id={"head": mate}, device_id_type=MESH,
        ).wait_recv()
    for g in range(GROUPS):
        rows_out[0, pl.ds(g, 32, stride=8), :] = back[g, 0:32].astype(F32)
        rows_out[1, pl.ds(g, 32, stride=8), :] = back[g, 32:64].astype(F32)
    store(rows_out.at[0], gk_hbm)
    store(rows_out.at[1], gq_hbm)

    for copy in gathers + forwards + sa_copies + io_copies + tot_copies + mate_copies + back_copies:
        copy.wait_send()
    for copy in stores:
        copy.wait()


def store_kernel(*refs):
    ins, outs, held, sems = refs[:6], refs[6:11], refs[11:18], refs[18]
    order = (4, 5, 0, 1, 2, 3)
    loads = [pltpu.make_async_copy(ins[i], held[i], sems.at[i]) for i in range(6)]
    for i in order:
        loads[i].start()
    loads[4].wait()
    loads[5].wait()
    tot, prior_w, gp = held[4], held[5], held[6]
    stores = []
    for k in range(4):
        for h in range(LOC):
            piece = tot[4 * h : 4 * h + 4].reshape(64, N).astype(F32)
            gp[k, 64 * h : 64 * h + 64, :] = prior_w[8 * k + h : 8 * k + h + 1, :] * piece
        stores.append(pltpu.make_async_copy(gp.at[k], outs[4].at[k], sems.at[6 + k]))
        stores[-1].start()
    for i in range(4):
        loads[i].wait()
        stores.append(pltpu.make_async_copy(held[i], outs[i], sems.at[10 + i]))
        stores[-1].start()
    for copy in stores:
        copy.wait()


def per_device(values, group_keys, group_queries, level_table, window_index, prior_states, cotangent):
    hbm = pl.BlockSpec(memory_space=pltpu.HBM)
    dma = pltpu.SemaphoreType.DMA
    wide, narrow = jax.ShapeDtypeStruct((TOK, HP), BF), jax.ShapeDtypeStruct((256, N), F32)
    parts = pl.pallas_call(
        kernel,
        out_shape=(
            wide, wide, narrow, narrow,
            jax.ShapeDtypeStruct((NS, 16, N), BF),
            jax.ShapeDtypeStruct((32, N), F32),
        ),
        in_specs=[hbm] * 7,
        out_specs=(hbm,) * 6,
        scratch_shapes=[
            pltpu.SMEM((LOC, 20), jnp.int32),
            pltpu.SMEM((1,), jnp.int32),
            pltpu.VMEM((TOK, HP), BF),
            pltpu.VMEM((TOK, HP), BF),
            pltpu.VMEM((256, N), BF),
            pltpu.VMEM((256, N), BF),
            pltpu.VMEM((4, 16, N), BF),
            pltpu.VMEM((HP, TOK), BF),
            pltpu.VMEM((HP, TOK), BF),
            pltpu.VMEM((GROUPS, 64, N), BF),
            pltpu.VMEM((NH, 64, N), BF),
            pltpu.VMEM((LOC, 128, 128), F32),
            pltpu.VMEM((LOC, 128, 128), F32),
            pltpu.VMEM((4, 128, 128), BF),
            pltpu.VMEM((2, 128, 128), BF),
            pltpu.VMEM((256, 256), BF),
            pltpu.VMEM((NS, 2, 16, N), BF),
            pltpu.VMEM((NS, 2, 16, N), BF),
            pltpu.VMEM((NS, 2, 16, N), BF),
            pltpu.VMEM((NS, 2, 16, N), BF),
            pltpu.VMEM((16, N), BF),
            pltpu.VMEM((NS, 16, N), BF),
            pltpu.VMEM((TOK, HP), F32),
            pltpu.VMEM((TOK, HP), F32),
            pltpu.VMEM((NH, 64, N), F32),
            pltpu.VMEM((NH, 64, N), BF),
            pltpu.VMEM((8, 64, N), BF),
            pltpu.VMEM((8, 64, N), BF),
            pltpu.VMEM((GROUPS, 64, N), BF),
            pltpu.VMEM((2, TOK, HP), BF),
            pltpu.VMEM((2, 256, N), F32),
            pltpu.VMEM((32, N), F32),
            dma((13,)),
            dma((GROUPS,)),
            dma((NH,)),
            dma((7,)),
            dma((NS,)),
            dma((NS,)),
            dma((NS,)),
            dma((NS,)),
            dma((NS,)),
            dma((NS,)),
            dma((8,)),
            dma((8,)),
            dma((8,)),
            dma((8,)),
        ],
        compiler_params=pltpu.CompilerParams(
            collective_id=0, has_side_effects=True, vmem_limit_bytes=62 * 1024 * 1024
        ),
    )(
        values,
        group_keys.reshape(256, N),
        group_queries.reshape(256, N),
        level_table,
        window_index,
        prior_states.reshape(4, HP, N),
        cotangent,
    )
    outs = pl.pallas_call(
        store_kernel,
        out_shape=(wide, wide, narrow, narrow, jax.ShapeDtypeStruct((4, HP, N), F32)),
        in_specs=[hbm] * 6,
        out_specs=(hbm,) * 5,
        scratch_shapes=[
            pltpu.VMEM((TOK, HP), BF),
            pltpu.VMEM((TOK, HP), BF),
            pltpu.VMEM((256, N), F32),
            pltpu.VMEM((256, N), F32),
            pltpu.VMEM((NS, 16, N), BF),
            pltpu.VMEM((32, N), F32),
            pltpu.VMEM((4, HP, N), F32),
            dma((14,)),
        ],
        compiler_params=pltpu.CompilerParams(vmem_limit_bytes=62 * 1024 * 1024),
    )(*parts)
    mixer_out, grad_values, grad_keys, grad_queries, grad_prior = outs
    return (
        mixer_out,
        grad_values,
        grad_keys.reshape(32, GROUPS, N),
        grad_queries.reshape(32, GROUPS, N),
        grad_prior.reshape(4, LOC, 64, N),
    )


def solution(mesh):
    rows = P(("seq", "head"), None, None)
    return jax.shard_map(
        per_device,
        mesh=mesh,
        in_specs=(P("seq", "head"), rows, rows, P("head", None), P(), P(None, "head", None, None), P("seq", "head")),
        out_specs=(P("seq", "head"), P("seq", "head"), rows, rows, P(None, "head", None, None)),
        check_vma=False,
    )
```

```python
import jax
import jax.numpy as jnp
from jax import lax
from jax.experimental import pallas as pl
from jax.experimental.pallas import tpu as pltpu
from jax.sharding import PartitionSpec as P

HEADS = 128
GROUPS = 8
NS = 32
NH = 16
TOK = 512
HP = 512
LOC = 8
N = 128
BF = jnp.bfloat16
F32 = jnp.float32
MESH = pl.DeviceIdType.MESH

NN = (((1,), (0,)), ((), ()))
NT = (((1,), (1,)), ((), ()))
TN = (((0,), (0,)), ((), ()))


def mm(a, b, dims=NN):
    return lax.dot_general(a, b, dims, preferred_element_type=F32)


def root(level):
    return float(2.0 ** (-max(level - 1, 0) / 2))


def hops():
    rel = [(dy, dx, dc) for dy in range(4) for dx in range(4) for dc in range(2)]
    rel.remove((0, 0, 0))
    near = lambda a: min(a, 4 - a)
    rel.sort(key=lambda r: -(near(r[0]) + near(r[1])))
    return rel


def kernel(
    v_hbm, k_hbm, q_hbm, table_hbm, window_hbm, prior_hbm, c_hbm,
    mix_hbm, gv_hbm, gk_hbm, gq_hbm, tot_hbm, prior_w_hbm,
    table, window, v, c, kraw, qraw, prior, vt, ct, kq_send, kq, factor, factor_t,
    g_diag, g_8, g_9, sa_send, sa_recv, io_send, io_recv,
    mix, gval, grad, mate_send, mate_recv, out_send, back, outs, rows_out, prior_w,
    local_sem, gat_send, gat_recv, fwd_send, sa_ss, sa_rs, io_ss, io_rs,
    mt_ss, mt_rs, bk_ss, bk_rs,
):
    me = lax.axis_index("seq")
    z = lax.axis_index("head")
    pair = lax.div(z, 2)
    odd = lax.rem(z, 2)
    sgn = 2 * odd - 1
    mate = z - sgn
    ring = lambda i: lax.rem(i + 2 * NH, NH)
    core, xx, yy = lax.rem(me, 2), lax.rem(lax.div(me, 2), 4), lax.div(me, 8)

    def seq_of(rel):
        dy, dx, dc = rel
        dy, dx = dy + core * ((4 - dy) % 4 - dy), dx + core * ((4 - dx) % 4 - dx)
        return lax.rem(yy + dy, 4) * 8 + lax.rem(xx + dx, 4) * 2 + lax.rem(core + dc, 2)

    relative = hops()
    near_z = [ring(z + sgn * j) for j in range(1, 8)]
    far_z = [ring(z - sgn * j) for j in (2, 4, 6)]

    barrier = pltpu.get_barrier_semaphore()
    for other in near_z + far_z + [mate]:
        pl.semaphore_signal(barrier, inc=1, device_id={"head": other}, device_id_type=MESH)
    for rel in relative:
        pl.semaphore_signal(barrier, inc=1, device_id={"seq": seq_of(rel)}, device_id_type=MESH)

    loads = [
        pltpu.make_async_copy(k_hbm, kraw, local_sem.at[0]),
        pltpu.make_async_copy(q_hbm, qraw, local_sem.at[1]),
        pltpu.make_async_copy(v_hbm, v, local_sem.at[2]),
        pltpu.make_async_copy(c_hbm, c, local_sem.at[3]),
        pltpu.make_async_copy(prior_hbm.at[:, pl.ds(pl.multiple_of(me * 16, 16), 16), :], prior, local_sem.at[4]),
        pltpu.make_async_copy(table_hbm, table, local_sem.at[11]),
        pltpu.make_async_copy(window_hbm, window, local_sem.at[12]),
    ]
    for load in loads:
        load.start()

    out_row = lax.broadcasted_iota(jnp.int32, (256, 256), 0)
    in_row = lax.broadcasted_iota(jnp.int32, (256, 256), 1)
    pick = (in_row == (out_row & 31) * 8 + (out_row >> 5)).astype(F32).astype(BF)
    loads[0].wait()
    k_sorted = mm(pick, kraw[...]).astype(BF)
    loads[1].wait()
    q_sorted = mm(pick, qraw[...]).astype(BF)
    for g in range(GROUPS):
        kq_send[g, 0:32, :] = k_sorted[32 * g : 32 * g + 32, :]
        kq_send[g, 32:64, :] = q_sorted[32 * g : 32 * g + 32, :]
    kq[z] = kq_send[pair]

    loads[5].wait()
    weight = lambda h, l: table[h, l].astype(F32) * root(l)
    row = lax.broadcasted_iota(jnp.int32, (128, 128), 0)
    col = lax.broadcasted_iota(jnp.int32, (128, 128), 1)
    spread = row ^ col
    for h in range(LOC):
        grid = jnp.full((128, 128), weight(h, 7), F32)
        for l in range(6, -1, -1):
            grid = jnp.where(spread < (1 << l), weight(h, l), grid)
        factor[h] = jnp.where(row >= col, grid, 0.0)
        factor_t[h] = jnp.where(col >= row, grid, 0.0)

    lane = lax.broadcasted_iota(jnp.int32, (1, HP), 1) >> 6

    def lanes_of(level):
        w = jnp.zeros((1, HP), F32)
        for h in range(LOC):
            w = jnp.where(lane == h, weight(h, level), w)
        return w

    w8, w9 = lanes_of(8), lanes_of(9)
    low_half = lax.broadcasted_iota(jnp.int32, (128, 128), 1) < 64

    def both(ref, i, pr):
        tile = ref[128 * i : 128 * i + 128, 128 * pr : 128 * pr + 128]
        zero = jnp.zeros_like(tile)
        return jnp.concatenate([jnp.where(low_half, tile, zero), jnp.where(low_half, zero, tile)], axis=0)

    loads[2].wait()
    loads[3].wait()
    vt[...] = v[...].T
    ct[...] = c[...].T

    def wide_grads():
        g_9[...] = mm((c[256:512, :].astype(F32) * w9).astype(BF), v[0:256, :], NT).astype(BF)
        for i in range(2):
            at = 256 * i
            g_8[i] = mm((c[at + 128 : at + 256, :].astype(F32) * w8).astype(BF), v[at : at + 128, :], NT).astype(BF)

    def diagonal_grads(i):
        total = jnp.zeros((128, 128), F32)
        for pr in range(4):
            raw = mm(both(c, i, pr), v[128 * i : 128 * i + 128, 128 * pr : 128 * pr + 128], NT)
            total = total + factor[2 * pr] * raw[:128] + factor[2 * pr + 1] * raw[128:]
        g_diag[i] = total.astype(BF)

    pl.semaphore_wait(barrier, 11 + 31)

    def gather_copy(block, to):
        return pltpu.make_async_remote_copy(
            src_ref=kq_send.at[block], dst_ref=kq.at[z], send_sem=gat_send.at[block], recv_sem=gat_recv.at[z],
            device_id={"head": to}, device_id_type=MESH,
        )

    opposite = lax.rem(pair + 4, 8)
    gathers = [gather_copy(opposite, 2 * opposite + 1 - odd)]
    for k in (3, 2, 1):
        right, left = lax.rem(pair + k, 8), lax.rem(pair + 8 - k, 8)
        gathers += [gather_copy(right, 2 * right), gather_copy(left, 2 * left + 1)]
    gathers.append(gather_copy(pair, mate))
    for copy in gathers:
        copy.start()

    wide_grads()
    for i in range(4):
        diagonal_grads(i)

    forwards = []
    for j in range(7):
        src = near_z[j]
        pltpu.make_async_remote_copy(
            src_ref=kq.at[src], dst_ref=kq.at[src], send_sem=gat_send.at[0], recv_sem=gat_recv.at[src],
            device_id={"head": mate}, device_id_type=MESH,
        ).wait_recv()
        forward = pltpu.make_async_remote_copy(
            src_ref=kq.at[src], dst_ref=kq.at[src], send_sem=fwd_send.at[j], recv_sem=gat_recv.at[src],
            device_id={"head": mate}, device_id_type=MESH,
        )
        forward.start()
        forwards.append(forward)
    for src in [mate] + [ring(mate - sgn * j) for j in range(1, 8)]:
        pltpu.make_async_remote_copy(
            src_ref=kq.at[src], dst_ref=kq.at[src], send_sem=gat_send.at[0], recv_sem=gat_recv.at[src],
            device_id={"head": mate}, device_id_type=MESH,
        ).wait_recv()

    keys = kq[:, 0:32, :].reshape(TOK, N)
    queries = kq[:, 32:64, :].reshape(TOK, N)

    sa_send[:, 0] = mm(vt[...], keys).astype(BF).reshape(NS, 16, N)
    sa_send[:, 1] = mm(ct[...], queries).astype(BF).reshape(NS, 16, N)

    def spread_out(src, dst, ss, rs):
        copies = []
        for n, rel in enumerate(relative):
            to = seq_of(rel)
            copies.append(pltpu.make_async_remote_copy(
                src_ref=src.at[to], dst_ref=dst.at[me], send_sem=ss.at[n], recv_sem=rs.at[me],
                device_id={"seq": to}, device_id_type=MESH,
            ))
        for copy in copies:
            copy.start()
        return copies

    def arrive(dst, ss, rs):
        for rel in relative:
            frm = seq_of(rel)
            pltpu.make_async_remote_copy(
                src_ref=dst.at[frm], dst_ref=dst.at[frm], send_sem=ss.at[0], recv_sem=rs.at[frm],
                device_id={"seq": frm}, device_id_type=MESH,
            ).wait_recv()

    sa_copies = spread_out(sa_send, sa_recv, sa_ss, sa_rs)
    sa_recv[me] = sa_send[me]

    def block(i):
        return slice(128 * i, 128 * i + 128)

    def inner_outputs():
        for i in range(4):
            q_i, k_i = queries[block(i)], keys[block(i)]
            score, score_t = mm(q_i, k_i, NT), mm(k_i, q_i, NT)
            for pr in range(4):
                cols = slice(128 * pr, 128 * pr + 128)
                w = jnp.concatenate([(factor[2 * pr] * score).astype(BF), (factor[2 * pr + 1] * score).astype(BF)], axis=1)
                mix[block(i), cols] = mm(w, both(v, i, pr))
                w = jnp.concatenate([(factor_t[2 * pr] * score_t).astype(BF), (factor_t[2 * pr + 1] * score_t).astype(BF)], axis=1)
                gval[block(i), cols] = mm(w, both(c, i, pr))
        for i in range(2):
            lo, hi = block(2 * i), block(2 * i + 1)
            mix[hi, :] += w8 * mm(mm(queries[hi], keys[lo], NT).astype(BF), v[lo, :])
            gval[lo, :] += w8 * mm(mm(keys[lo], queries[hi], NT).astype(BF), c[hi, :])
        lo, hi = slice(0, 256), slice(256, 512)
        mix[hi, :] += w9 * mm(mm(queries[hi], keys[lo], NT).astype(BF), v[lo, :])
        gval[lo, :] += w9 * mm(mm(keys[lo], queries[hi], NT).astype(BF), c[hi, :])

    def inner_grads():
        for i in range(4):
            gq = mm(g_diag[i], keys[block(i)])
            gk = mm(g_diag[i], queries[block(i)], TN)
            if i % 2 == 1:
                gq = gq + mm(g_8[i // 2], keys[block(i - 1)])
            else:
                gk = gk + mm(g_8[i // 2], queries[block(i + 1)], TN)
            if i >= 2:
                gq = gq + mm(g_9[128 * (i - 2) : 128 * (i - 1), :], keys[0:256])
            else:
                gk = gk + mm(g_9[:, 128 * i : 128 * (i + 1)], queries[256:512], TN)
            grad[4 * i : 4 * i + 4, 0:32] = gk.reshape(4, 32, N)
            grad[4 * i : 4 * i + 4, 32:64] = gq.reshape(4, 32, N)

    inner_grads()

    arrive(sa_recv, sa_ss, sa_rs)
    my_head = lax.div(me, 4)
    seq_w = [table[my_head, 10 + b].astype(F32) * root(10 + b) for b in range(5)]
    bit = lambda k: ((window[0] >> k) & 1).astype(F32)
    loads[4].wait()
    loads[6].wait()
    start = jnp.zeros((16, N), F32)
    for k in range(4):
        start = start + (table[my_head, 15 + k].astype(F32) * root(15 + k) * bit(k)) * prior[k].astype(F32)

    def sums(which):
        levels = [[sa_recv[j, which].astype(F32) for j in range(NS)]]
        for _ in range(5):
            last = levels[-1]
            levels.append([last[2 * j] + last[2 * j + 1] for j in range(len(last) // 2)])
        return levels

    levels = sums(0)
    flow = [start]
    for b in range(4, -1, -1):
        flow = [x for j, f in enumerate(flow) for x in (f, f + seq_w[b] * levels[b][2 * j])]
    for j in range(NS):
        io_send[j, 0] = flow[j].astype(BF)
    levels = sums(1)
    flow = [jnp.zeros((16, N), F32)]
    for b in range(4, -1, -1):
        flow = [x for j, f in enumerate(flow) for x in (f + seq_w[b] * levels[b][2 * j + 1], f)]
    for j in range(NS):
        io_send[j, 1] = flow[j].astype(BF)
    io_send[:, 2] = jnp.broadcast_to(levels[5][0].astype(BF)[None], (32, 16, N))

    io_copies = spread_out(io_send, io_recv, io_ss, io_rs)
    io_recv[me] = io_send[me]

    inner_outputs()

    arrive(io_recv, io_ss, io_rs)
    inflow = io_recv[:, 0].reshape(HP, N)
    outflow = io_recv[:, 1].reshape(HP, N)
    grad[:, 0:32] = grad[:, 0:32] + mm(v[...], outflow).reshape(NH, 32, N)
    grad[:, 32:64] = grad[:, 32:64] + mm(c[...], inflow).reshape(NH, 32, N)
    mate_send[...] = grad[...].astype(BF)

    def owners(first):
        turn = lax.div(first + 6, NH) * (NH - first)
        return [ring(first + lax.rem(turn + i, 7)) for i in range(7)]

    mine = owners(ring(z - 7 * (1 - odd) + odd))
    mates = owners(ring(mate - 7 * odd + (1 - odd))) + [mate]
    mate_copies = []
    for j in range(8):
        mate_copies.append(pltpu.make_async_remote_copy(
            src_ref=mate_send.at[mates[j]], dst_ref=mate_recv.at[j], send_sem=mt_ss.at[j], recv_sem=mt_rs.at[j],
            device_id={"head": mate}, device_id_type=MESH,
        ))
    for copy in mate_copies:
        copy.start()

    def mate_arrive(j):
        pltpu.make_async_remote_copy(
            src_ref=mate_recv.at[j], dst_ref=mate_recv.at[j], send_sem=mt_ss.at[j], recv_sem=mt_rs.at[j],
            device_id={"head": mate}, device_id_type=MESH,
        ).wait_recv()

    back_copies = []
    for j in range(7):
        to = mine[j]
        mate_arrive(j)
        out_send[j] = (grad[to] + mate_recv[j].astype(F32)).astype(BF)
        copy = pltpu.make_async_remote_copy(
            src_ref=out_send.at[j], dst_ref=back.at[pair], send_sem=bk_ss.at[j], recv_sem=bk_rs.at[pair],
            device_id={"head": to}, device_id_type=MESH,
        )
        copy.start()
        back_copies.append(copy)
    mate_arrive(7)
    back[pair] = (grad[z] + mate_recv[7].astype(F32)).astype(BF)

    stores = []

    def store(src, dst):
        stores.append(pltpu.make_async_copy(src, dst, local_sem.at[5 + len(stores)]))
        stores[-1].start()

    outs[0] = (mix[...] + mm(queries, inflow, NT)).astype(BF)
    store(outs.at[0], mix_hbm)
    outs[1] = (gval[...] + mm(keys, outflow, NT)).astype(BF)
    store(outs.at[1], gv_hbm)
    for h in range(LOC):
        for k in range(4):
            prior_w[8 * k + h : 8 * k + h + 1, :] = jnp.full((1, N), weight(h, 15 + k) * bit(k), F32)
    store(prior_w, prior_w_hbm)
    store(io_recv.at[:, 2], tot_hbm)

    for k in range(1, 8):
        frm = lax.rem(pair + k, 8)
        pltpu.make_async_remote_copy(
            src_ref=back.at[frm], dst_ref=back.at[frm], send_sem=bk_ss.at[0], recv_sem=bk_rs.at[frm],
            device_id={"head": mate}, device_id_type=MESH,
        ).wait_recv()
    for g in range(GROUPS):
        rows_out[0, pl.ds(g, 32, stride=8), :] = back[g, 0:32].astype(F32)
        rows_out[1, pl.ds(g, 32, stride=8), :] = back[g, 32:64].astype(F32)
    store(rows_out.at[0], gk_hbm)
    store(rows_out.at[1], gq_hbm)

    for copy in gathers + forwards + sa_copies + io_copies + mate_copies + back_copies:
        copy.wait_send()
    for copy in stores:
        copy.wait()


def store_kernel(*refs):
    ins, outs, held, sems = refs[:6], refs[6:11], refs[11:18], refs[18]
    order = (4, 5, 0, 1, 2, 3)
    loads = [pltpu.make_async_copy(ins[i], held[i], sems.at[i]) for i in range(6)]
    for i in order:
        loads[i].start()
    loads[4].wait()
    loads[5].wait()
    tot, prior_w, gp = held[4], held[5], held[6]
    stores = []
    for k in range(4):
        for h in range(LOC):
            piece = tot[4 * h : 4 * h + 4].reshape(64, N).astype(F32)
            gp[k, 64 * h : 64 * h + 64, :] = prior_w[8 * k + h : 8 * k + h + 1, :] * piece
        stores.append(pltpu.make_async_copy(gp.at[k], outs[4].at[k], sems.at[6 + k]))
        stores[-1].start()
    for i in range(4):
        loads[i].wait()
        stores.append(pltpu.make_async_copy(held[i], outs[i], sems.at[10 + i]))
        stores[-1].start()
    for copy in stores:
        copy.wait()


def per_device(values, group_keys, group_queries, level_table, window_index, prior_states, cotangent):
    hbm = pl.BlockSpec(memory_space=pltpu.HBM)
    dma = pltpu.SemaphoreType.DMA
    wide, narrow = jax.ShapeDtypeStruct((TOK, HP), BF), jax.ShapeDtypeStruct((256, N), F32)
    parts = pl.pallas_call(
        kernel,
        out_shape=(
            wide, wide, narrow, narrow,
            jax.ShapeDtypeStruct((NS, 16, N), BF),
            jax.ShapeDtypeStruct((32, N), F32),
        ),
        in_specs=[hbm] * 7,
        out_specs=(hbm,) * 6,
        scratch_shapes=[
            pltpu.SMEM((LOC, 20), jnp.int32),
            pltpu.SMEM((1,), jnp.int32),
            pltpu.VMEM((TOK, HP), BF),
            pltpu.VMEM((TOK, HP), BF),
            pltpu.VMEM((256, N), BF),
            pltpu.VMEM((256, N), BF),
            pltpu.VMEM((4, 16, N), BF),
            pltpu.VMEM((HP, TOK), BF),
            pltpu.VMEM((HP, TOK), BF),
            pltpu.VMEM((GROUPS, 64, N), BF),
            pltpu.VMEM((NH, 64, N), BF),
            pltpu.VMEM((LOC, 128, 128), F32),
            pltpu.VMEM((LOC, 128, 128), F32),
            pltpu.VMEM((4, 128, 128), BF),
            pltpu.VMEM((2, 128, 128), BF),
            pltpu.VMEM((256, 256), BF),
            pltpu.VMEM((NS, 2, 16, N), BF),
            pltpu.VMEM((NS, 2, 16, N), BF),
            pltpu.VMEM((NS, 3, 16, N), BF),
            pltpu.VMEM((NS, 3, 16, N), BF),
            pltpu.VMEM((TOK, HP), F32),
            pltpu.VMEM((TOK, HP), F32),
            pltpu.VMEM((NH, 64, N), F32),
            pltpu.VMEM((NH, 64, N), BF),
            pltpu.VMEM((8, 64, N), BF),
            pltpu.VMEM((8, 64, N), BF),
            pltpu.VMEM((GROUPS, 64, N), BF),
            pltpu.VMEM((2, TOK, HP), BF),
            pltpu.VMEM((2, 256, N), F32),
            pltpu.VMEM((32, N), F32),
            dma((13,)),
            dma((GROUPS,)),
            dma((NH,)),
            dma((7,)),
            dma((NS,)),
            dma((NS,)),
            dma((NS,)),
            dma((NS,)),
            dma((8,)),
            dma((8,)),
            dma((8,)),
            dma((8,)),
        ],
        compiler_params=pltpu.CompilerParams(
            collective_id=0, has_side_effects=True, vmem_limit_bytes=62 * 1024 * 1024
        ),
    )(
        values,
        group_keys.reshape(256, N),
        group_queries.reshape(256, N),
        level_table,
        window_index,
        prior_states.reshape(4, HP, N),
        cotangent,
    )
    outs = pl.pallas_call(
        store_kernel,
        out_shape=(wide, wide, narrow, narrow, jax.ShapeDtypeStruct((4, HP, N), F32)),
        in_specs=[hbm] * 6,
        out_specs=(hbm,) * 5,
        scratch_shapes=[
            pltpu.VMEM((TOK, HP), BF),
            pltpu.VMEM((TOK, HP), BF),
            pltpu.VMEM((256, N), F32),
            pltpu.VMEM((256, N), F32),
            pltpu.VMEM((NS, 16, N), BF),
            pltpu.VMEM((32, N), F32),
            pltpu.VMEM((4, HP, N), F32),
            dma((14,)),
        ],
        compiler_params=pltpu.CompilerParams(vmem_limit_bytes=62 * 1024 * 1024),
    )(*parts)
    mixer_out, grad_values, grad_keys, grad_queries, grad_prior = outs
    return (
        mixer_out,
        grad_values,
        grad_keys.reshape(32, GROUPS, N),
        grad_queries.reshape(32, GROUPS, N),
        grad_prior.reshape(4, LOC, 64, N),
    )


def solution(mesh):
    rows = P(("seq", "head"), None, None)
    return jax.shard_map(
        per_device,
        mesh=mesh,
        in_specs=(P("seq", "head"), rows, rows, P("head", None), P(), P(None, "head", None, None), P("seq", "head")),
        out_specs=(P("seq", "head"), P("seq", "head"), rows, rows, P(None, "head", None, None)),
        check_vma=False,
    )
```
